32 devices in a mesh: rep: 4 (over z), fsdp: 2 (over x), ctx: 4 (over y, core).
Axes of the slice: x: 2, y: 2, z: 4, core: 2. Of those that a mesh axis runs over, the one named last changes fastest.
Arguments:
- q_proj: bfloat16 [16, 256, 4096], P(('rep', 'fsdp'), 'ctx'), may hold values from -24 to 24
- k_proj: bfloat16 [16, 256, 512], P(('rep', 'fsdp'), 'ctx'), may hold values from -24 to 24
- v_proj: bfloat16 [16, 256, 512], P(('rep', 'fsdp'), 'ctx'), may hold values from -6 to 6
- attn_out: bfloat16 [16, 256, 4096], P(('rep', 'fsdp'), 'ctx'), may hold values from -6 to 6
- upstream: bfloat16 [16, 256, 4096], P(('rep', 'fsdp'), 'ctx'), may hold values from -6 to 6
- advantage: float32 [16, 256], P(('rep', 'fsdp'), 'ctx'), may hold values from -4 to 4
- action_mask: int32 [16, 256], P(('rep', 'fsdp'), 'ctx'), may hold values 0 or 1
- segment_ids: int32 [16, 256], P(('rep', 'fsdp'), 'ctx'), may hold values from 0 to 3, never falling along the last dimension, each value on 1 to 128 neighbouring positions
- codebook: int32 [16, 256], P(('rep', 'fsdp'), 'ctx'), may hold values from 0 to 8, as said below
Outputs:
- grad_q: bfloat16 [16, 256, 4096], P(('rep', 'fsdp'), 'ctx')
- grad_k: bfloat16 [16, 256, 512], P(('rep', 'fsdp'), 'ctx')
- grad_v: bfloat16 [16, 256, 512], P(('rep', 'fsdp'), 'ctx')
- grad_bias_q: float32 [4096], P('fsdp')
- grad_bias_k: float32 [512], P('fsdp')
- grad_bias_v: float32 [512], P('fsdp')
The draws below stay inside these ranges and needn't reach their ends.
Inputs may be any that keep to these rules, and one draw needn't show every extreme that they name: `codebook`: tokens come in aligned blocks of 8 positions of a dialogue; each block is text (all 0) or one speech frame holding codebooks 1 to 8 in order.
All inputs are finite; a program needn't handle non-finite values. No bound on the sum of `action_mask` on one device may be relied on, other than what follows from the above.
Results may differ from the reference program's by a relative error of at most 0.012.
The reference program's roundings to bfloat16 on the way count: a program that leaves them out, or rounds other values in their place, can miss the bound.
Values may be sent and summed in bfloat16 or wider, within the bound.
A program may use at most 64 MiB of HBM per device.

```python
import math
import jax
import jax.numpy as jnp
import numpy as np
from jax import lax

HQ = 32
HK = 4
HD = 128
GROUP = 8
LEN = 256
NSEQ = 16


def draw_codebook(key, part):
    frames = LEN // 8
    block_index = jnp.arange(frames, dtype=jnp.int32)
    audio_limit = 900 - 800 * block_index // frames
    draw_bits = jax.random.randint(jax.random.fold_in(key, 11), (NSEQ, frames), 0, 1000)
    is_audio = draw_bits < audio_limit[None, :]
    frame_codes = jnp.arange(8, dtype=jnp.int32) + 1
    code_rows = jnp.where(is_audio[:, :, None], frame_codes[None, None, :], 0)
    return code_rows.reshape(NSEQ, LEN).astype(jnp.int32)


def attention_inputs(key):
    base_q = jax.random.normal(jax.random.fold_in(key, 21), (NSEQ, LEN, HQ, HD), jnp.float32)
    base_k = jax.random.normal(jax.random.fold_in(key, 22), (NSEQ, LEN, HK, HD), jnp.float32)
    keys_out = base_k
    queries_out = base_q
    queries_out = jnp.clip(queries_out, -24.0, 24.0).reshape(NSEQ, LEN, HQ * HD)
    keys_out = jnp.clip(keys_out, -24.0, 24.0).reshape(NSEQ, LEN, HK * HD)
    return (queries_out, keys_out)


def draw_q_proj(key, part):
    return attention_inputs(key)[0].astype(jnp.bfloat16)


def draw_k_proj(key, part):
    return attention_inputs(key)[1].astype(jnp.bfloat16)


def with_ends(values, stream_key, smallest, largest):
    index_at = [jax.random.randint(jax.random.fold_in(stream_key, axis), (), 0, length) for axis, length in enumerate(values.shape)]
    main_axis = values.shape.index(max(values.shape))
    neighbour = index_at[:main_axis] + [(index_at[main_axis] + 1) % values.shape[main_axis]] + index_at[main_axis + 1:]
    return values.at[tuple(index_at)].set(smallest).at[tuple(neighbour)].set(largest)


def raised(array, stream_key, source, target, blocks, factor):
    def block_of(axis_at):
        return (jnp.arange(array.shape[axis_at]) // (array.shape[axis_at] // blocks)).reshape((-1,) + (1,) * (array.ndim - 1 - axis_at))

    first = jax.random.permutation(stream_key, blocks)[block_of(target)]
    far = (block_of(target) + blocks // 2) % blocks
    return jnp.where((block_of(source) == first) | (block_of(source) == far), factor * array, array)


def levels(stream_key, dims, shards, low, top_value):
    factor_of, own = 1.0, jax.random.fold_in(stream_key, 6)
    for axis_at, shards_of in shards:
        draws = jnp.exp(jax.random.uniform(jax.random.fold_in(own, axis_at), (shards_of,), jnp.float32, low / len(shards), top_value / len(shards)))
        factor_of = factor_of * jnp.repeat(draws, dims[axis_at] // shards_of).reshape([-1 if axis == axis_at else 1 for axis in range(len(dims))])
    return factor_of


def profile(count, total, bound, lean):
    loads = [(1 << 20) // math.isqrt(standing ** lean) + 1 for standing in range(2, count + 1)]
    surplus, given = total - bound - (count - 1), [1] * (count - 1)
    while surplus > 0:
        candidates = [i for i in range(count - 1) if given[i] < bound]
        mass, budget = sum([loads[i] for i in candidates]), surplus
        for i in candidates:
            more = min(bound - given[i], max(1, budget * loads[i] // mass), surplus)
            given[i] = given[i] + more
            surplus = surplus - more
    return np.array([bound] + given)


def uneven(own_key, amount, total, bound, skew):
    if amount == 2:
        one = jax.random.randint(own_key, (), max(1, total - bound), min(bound, total - 1) + 1)
        return jnp.stack([one, total - one])
    tallies = jnp.asarray(profile(amount, total, bound, skew), jnp.int32)
    pairs = (amount - 1) // 2
    source_of, sink = tallies[1:1 + 2 * pairs:2], tallies[2:2 + 2 * pairs:2]
    slack = jnp.minimum(source_of - 1, bound - sink)
    passed = jax.random.randint(jax.random.fold_in(own_key, 1), (pairs,), 0, 1 << 20) % (slack + 1)
    tallies = tallies.at[1:1 + 2 * pairs:2].set(source_of - passed).at[2:2 + 2 * pairs:2].set(sink + passed)
    return tallies[jax.random.permutation(jax.random.fold_in(own_key, 2), amount)]


def noise(stream_key, extent, spread, limit, cuts=(), kind=jnp.bfloat16):
    factor_of = levels(stream_key, extent, cuts, -0.22, 0.18) if cuts else 1.0
    result = jax.random.normal(stream_key, extent, jnp.float32) * spread * factor_of
    return jnp.minimum(jnp.maximum(result, -limit), limit).astype(kind)


def gaussian_with(stream_key, extent, width, limit, cuts, heavy, kind=jnp.bfloat16):
    result = width * jax.random.normal(stream_key, extent, jnp.float32)
    if cuts:
        result = result * levels(stream_key, extent, cuts, -0.22, 0.18)
    return jnp.clip(raised(result, jax.random.fold_in(stream_key, 3), *heavy), -limit, limit).astype(kind)


def setup_inputs(seed: int = 0) -> dict:
    arg_keys = jax.random.split(jax.random.key(seed), 10)
    return {
        "q_proj": draw_q_proj(jax.random.fold_in(arg_keys[9], 71), 0),
        "k_proj": draw_k_proj(jax.random.fold_in(arg_keys[9], 71), 0),
        "v_proj": noise(arg_keys[2], (NSEQ, LEN, HK * HD), 1.0, 6.0, ((0, 8), (1, 4))),
        "attn_out": noise(arg_keys[3], (NSEQ, LEN, HQ * HD), 1.0, 6.0, ((0, 8), (1, 4))),
        "upstream": gaussian_with(arg_keys[4], (NSEQ, LEN, HQ * HD), 1.0, 6.0, ((0, 8), (1, 4)), (0, 2, 8, 2.0)),
        "advantage": noise(arg_keys[5], (NSEQ, LEN), 1.0, 4.0, ((0, 8), (1, 4)), jnp.float32),
        "action_mask": with_ends((jax.random.randint(arg_keys[6], (NSEQ, LEN), 0, 3) < 2).astype(jnp.int32), jax.random.fold_in(arg_keys[6], 1), 0, 1),
        "segment_ids": jax.vmap(lambda own: jnp.searchsorted(jnp.cumsum(uneven(own, 4, LEN, LEN // 2, 1)), jnp.arange(LEN), side="right"))(jax.random.split(arg_keys[7], NSEQ)).reshape((NSEQ, LEN)).astype(jnp.int32),
        "codebook": draw_codebook(jax.random.fold_in(arg_keys[9], 71), 0),
    }


ROPE_BASE = 1000000.0


def rotary_tables(positions):
    half_width = HD // 2
    steps = jnp.arange(half_width, dtype=jnp.float32)
    inverse = jnp.exp(steps * (-2.0 * math.log(ROPE_BASE) / HD))
    angles = positions.astype(jnp.float32)[..., None] * inverse
    return jnp.cos(angles), jnp.sin(angles)


def rotate(inputs, cosine_table, sine_table):
    half_width = inputs.shape[-1] // 2
    first_half = inputs[..., :half_width]
    second = inputs[..., half_width:]
    cos_rows = cosine_table[..., None, :]
    sin_rows = sine_table[..., None, :]
    return jnp.concatenate([first_half * cos_rows - second * sin_rows, second * cos_rows + first_half * sin_rows], axis=-1)


def one_sequence(pieces_in):
    q_seq, k_seq, v_seq, o_seq, up_seq, adv_seq, mask_seq, seg_seq, code_seq = pieces_in
    positions = jnp.cumsum((code_seq <= 1).astype(jnp.int32)) - 1
    cosine_table, sine_table = rotary_tables(positions)
    q_rot = rotate(q_seq.reshape(LEN, HQ, HD).astype(jnp.float32), cosine_table, sine_table).astype(jnp.bfloat16)
    k_rot = rotate(k_seq.reshape(LEN, HK, HD).astype(jnp.float32), cosine_table, sine_table).astype(jnp.bfloat16)
    weight = adv_seq * mask_seq.astype(jnp.float32)
    grad_out = (weight[:, None] * up_seq.astype(jnp.float32)).astype(jnp.bfloat16).reshape(LEN, HQ, HD)
    delta_rows = jnp.sum(grad_out.astype(jnp.float32) * o_seq.reshape(LEN, HQ, HD).astype(jnp.float32), axis=-1)
    row_index = jnp.arange(LEN)
    allowed = (seg_seq[:, None] == seg_seq[None, :]) & (row_index[None, :] <= row_index[:, None])
    softmax_scale = HD ** -0.5
    value_rows = v_seq.reshape(LEN, HK, HD)

    def one_group(state_value, group_index):
        start = (group_index * GROUP).astype(jnp.int32)
        q_group = lax.dynamic_slice_in_dim(q_rot, start, GROUP, 1).astype(jnp.float32)
        g_group = lax.dynamic_slice_in_dim(grad_out, start, GROUP, 1).astype(jnp.float32)
        d_group = lax.dynamic_slice_in_dim(delta_rows, start, GROUP, 1)
        k_group = lax.dynamic_index_in_dim(k_rot, group_index, 1, False).astype(jnp.float32)
        v_group = lax.dynamic_index_in_dim(value_rows, group_index, 1, False).astype(jnp.float32)
        scores = jnp.einsum("qhd,kd->hqk", q_group, k_group) * softmax_scale
        scores = jnp.where(allowed[None], scores, -jnp.inf)
        row_max = jnp.max(scores, axis=2, keepdims=True)
        row_total = jnp.sum(jnp.exp(scores - row_max), axis=2, keepdims=True)
        attention = jnp.exp(scores - (row_max + jnp.log(row_total)))
        attention_reduced_precision = lax.optimization_barrier(attention.astype(jnp.bfloat16)).astype(jnp.float32)
        grad_v_part = jnp.einsum("hqk,qhd->kd", attention_reduced_precision, g_group)
        grad_probs = jnp.einsum("qhd,kd->hqk", g_group, v_group)
        scores_gradient = attention * (grad_probs - jnp.transpose(d_group)[:, :, None])
        grad_scores_low = lax.optimization_barrier(scores_gradient.astype(jnp.bfloat16)).astype(jnp.float32)
        grad_q_part = jnp.einsum("hqk,kd->qhd", grad_scores_low, k_group) * softmax_scale
        grad_k_part = jnp.einsum("hqk,qhd->kd", grad_scores_low, q_group) * softmax_scale
        return state_value, (grad_q_part, grad_k_part, grad_v_part)

    _, (grad_q_groups, grad_k_groups, grad_v_groups) = lax.scan(one_group, jnp.int32(0), jnp.arange(HK, dtype=jnp.int32))
    grad_q_rot = jnp.transpose(grad_q_groups, (1, 0, 2, 3)).reshape(LEN, HQ, HD)
    grad_k_rot = jnp.transpose(grad_k_groups, (1, 0, 2))
    grad_v_acc = jnp.transpose(grad_v_groups, (1, 0, 2))
    grad_q_seq = rotate(grad_q_rot, cosine_table, -sine_table).astype(jnp.bfloat16).reshape(LEN, HQ * HD)
    grad_k_seq = rotate(grad_k_rot, cosine_table, -sine_table).astype(jnp.bfloat16).reshape(LEN, HK * HD)
    grad_v_seq = grad_v_acc.astype(jnp.bfloat16).reshape(LEN, HK * HD)
    return grad_q_seq, grad_k_seq, grad_v_seq


def reference(q_proj, k_proj, v_proj, attn_out, upstream, advantage, action_mask, segment_ids, codebook):
    grad_q, grad_k, grad_v = lax.map(one_sequence, (q_proj, k_proj, v_proj, attn_out, upstream, advantage, action_mask, segment_ids, codebook))
    grad_bias_q = jnp.sum(grad_q.astype(jnp.float32), axis=(0, 1))
    grad_bias_k = jnp.sum(grad_k.astype(jnp.float32), axis=(0, 1))
    grad_bias_v = jnp.sum(grad_v.astype(jnp.float32), axis=(0, 1))
    return (grad_q, grad_k, grad_v, grad_bias_q, grad_bias_k, grad_bias_v)
```

```python
import functools
import math

import jax
import jax.numpy as jnp
from jax import lax
from jax.experimental import pallas as pl
from jax.experimental.pallas import tpu as pltpu
from jax.sharding import PartitionSpec as P

HQ = 32
HK = 4
HD = 128
GROUP = HQ // HK
ROPE_BASE = 1000000.0
F32 = jnp.float32
BF16 = jnp.bfloat16
MESH = pl.DeviceIdType.MESH
NT = (((1,), (1,)), ((), ()))
TN = (((0,), (0,)), ((), ()))


def bias_layout(fsdps):
    q_rows, kv_rows = HQ // fsdps, max(1, HK // fsdps)
    return q_rows, kv_rows, -(-(q_rows + 2 * kv_rows) // 8) * 8


def rope(x, cos, sin):
    return x * cos + pltpu.roll(x, HD // 2, 1) * sin


def kernel(
    sizes,
    q_hbm, k_hbm, v_hbm, o_hbm, up_hbm, adv_ref, act_ref, seg_ref, code_ref,
    gq_hbm, gk_ref, gv_ref, bq_ref, bk_ref, bv_ref,
    q_in, o_in, up_in, k_all, v_all, code_all, seg_all,
    q_rot, g_low, delta, cos_tab, sin_tab, mask_tab,
    gq_out, part, own, exch, sums, arrive, bias_q, bias, bias_in, bias_half, bias_half_in,
    in_sem, out_sem, meta_send, meta_recv, kv_send, kv_recv, fw_send, fw_recv,
    ex_send, ex_recv, cr_send, cr_recv, b1_send, b1_recv, b2_send, b2_recv,
):
    n, reps, fsdps, seqs, toks = sizes
    length = n * toks
    pairs = n // 2
    chunks = seqs * HK
    width = GROUP * HD
    lanes = GROUP * toks
    scale = HD ** -0.5
    me = lax.axis_index("ctx")
    rep = lax.axis_index("rep")
    fs = lax.axis_index("fsdp")
    pair = me // 2
    core = me % 2
    buddy = me + 1 - 2 * core
    here = rep * fsdps + fs
    others = reps * fsdps
    q_rows, kv_rows, bias_rows = bias_layout(fsdps)

    def ctx_device(index):
        return {"ctx": index}

    def far_device(step):
        target = (here + step) % others
        return {"rep": target // fsdps, "fsdp": target % fsdps}

    def rows(index):
        return pl.ds(pl.multiple_of(index * toks, toks), toks)

    def cols(group):
        return pl.ds(pl.multiple_of(group * HD, HD), HD)

    def wide(group):
        return pl.ds(pl.multiple_of(group * width, width), width)

    loads = []
    for seq in range(seqs):
        loads.append(pltpu.make_async_copy(up_hbm.at[seq], up_in.at[seq], in_sem.at[0, seq]))
        loads.append(pltpu.make_async_copy(o_hbm.at[seq], o_in.at[seq], in_sem.at[1, seq]))
    for seq in range(seqs):
        loads.append(pltpu.make_async_copy(q_hbm.at[seq], q_in.at[seq], in_sem.at[2, seq]))
        loads.append(pltpu.make_async_copy(k_hbm.at[seq], k_all.at[seq, rows(me)], in_sem.at[3, seq]))
        loads.append(pltpu.make_async_copy(v_hbm.at[seq], v_all.at[seq, rows(me)], in_sem.at[4, seq]))
    for load in loads:
        load.start()

    barrier = pltpu.get_barrier_semaphore()
    for step in range(1, n):
        pl.semaphore_signal(barrier, inc=1, device_id=ctx_device((me + step) % n), device_id_type=MESH)
    for step in range(1, others):
        pl.semaphore_signal(barrier, inc=1, device_id=far_device(step), device_id_type=MESH)

    def clear(index, _):
        for seq in range(seqs):
            k_all[seq, rows(index), :] = jnp.zeros((toks, HK * HD), BF16)
            v_all[seq, rows(index), :] = jnp.zeros((toks, HK * HD), BF16)
        code_all[index] = jnp.zeros((seqs, toks), jnp.int32)
        seg_all[index] = jnp.zeros((seqs, toks), jnp.int32)
        return 0

    lax.fori_loop(me + 1, n, clear, 0)
    code_all[me] = code_ref[...]
    seg_all[me] = seg_ref[...]

    pl.semaphore_wait(barrier, n - 1 + others - 1)

    def meta_copy(source, target, slot):
        a = pltpu.make_async_remote_copy(
            code_ref, code_all.at[source], meta_send.at[0, slot], meta_recv.at[0, source],
            device_id=ctx_device(target), device_id_type=MESH)
        b = pltpu.make_async_remote_copy(
            seg_ref, seg_all.at[source], meta_send.at[1, slot], meta_recv.at[1, source],
            device_id=ctx_device(target), device_id_type=MESH)
        return a, b

    def meta_start(target, _):
        for copy in meta_copy(me, target, target):
            copy.start()
        return 0

    lax.fori_loop(me + 1, n, meta_start, 0)

    def kv_copy(source, target, slot, chunk, send, recv, forward):
        seq, group = chunk // HK, chunk % HK
        made = []
        for kind, (hbm, held) in enumerate(((k_hbm, k_all), (v_hbm, v_all))):
            place = held.at[seq, rows(source), cols(group)]
            origin = place if forward else hbm.at[seq, :, cols(group)]
            made.append(pltpu.make_async_remote_copy(
                origin, place, send.at[kind, slot, chunk], recv.at[kind, source, chunk],
                device_id=ctx_device(target), device_id_type=MESH))
        return made

    def kv_start(chunk, _):
        def later(other, _):
            for copy in kv_copy(me, 2 * other + core, other, chunk, kv_send, kv_recv, False):
                copy.start()
            return 0

        lax.fori_loop(pair + 1, pairs, later, 0)

        @pl.when(core == 0)
        def _():
            for copy in kv_copy(me, buddy, pair, chunk, kv_send, kv_recv, False):
                copy.start()
        return 0

    lax.fori_loop(0, chunks, kv_start, 0)

    eye = lax.broadcasted_iota(jnp.int32, (toks, toks), 0) == lax.broadcasted_iota(
        jnp.int32, (toks, toks), 1)

    def column(row):
        return jnp.sum(jnp.where(eye, row, 0.0), axis=1, keepdims=True)

    weight_rows = adv_ref[...] * act_ref[...].astype(F32)
    ones = jnp.ones((8, HD), BF16)
    for seq in range(seqs):
        weight = column(weight_rows[seq:seq + 1, :])
        loads[2 * seq].wait()
        loads[2 * seq + 1].wait()

        def cotangent(group, _, seq=seq, weight=weight):
            chunk = seq * HK + group
            up = up_in[seq, :, wide(group)]
            out = o_in[seq, :, wide(group)]
            high, low = [], []
            for head in range(GROUP):
                part_cols = slice(head * HD, (head + 1) * HD)
                rounded = (weight * up[:, part_cols].astype(F32)).astype(BF16)
                g_low[chunk, head * toks:(head + 1) * toks, :] = rounded
                product = rounded.astype(F32) * out[:, part_cols].astype(F32)
                top = product.astype(BF16)
                high.append(top)
                low.append((product - top.astype(F32)).astype(BF16))
            total = lax.dot_general(ones, jnp.concatenate(high, axis=0), NT, preferred_element_type=F32)
            total += lax.dot_general(ones, jnp.concatenate(low, axis=0), NT, preferred_element_type=F32)
            delta[chunk] = total
            return 0

        lax.fori_loop(0, HK, cotangent, 0)

    def meta_wait(source, _):
        for copy in meta_copy(source, me, 0):
            copy.wait_recv()
        return 0

    lax.fori_loop(0, me, meta_wait, 0)
    row_of = lax.broadcasted_iota(jnp.int32, (length, toks), 0)
    col_of = lax.broadcasted_iota(jnp.int32, (length, toks), 1)
    lane = lax.broadcasted_iota(jnp.int32, (1, HD), 1)
    first = lane < HD // 2
    key_index = lax.broadcasted_iota(jnp.int32, (length, lanes), 0)
    query_index = lax.broadcasted_iota(jnp.int32, (length, lanes), 1) % toks + me * toks
    causal = key_index <= query_index
    spread = (lax.broadcasted_iota(jnp.int32, (toks, lanes), 0)
              == lax.broadcasted_iota(jnp.int32, (toks, lanes), 1) % toks).astype(F32)
    position = []
    for seq in range(seqs):
        count = jnp.zeros((length, toks), F32)
        seg_columns = []
        for block in range(n):
            starts = jnp.where(code_all[block][seq:seq + 1, :] <= 1, 1.0, 0.0)
            count = count + jnp.where(col_of + block * toks <= row_of, starts, 0.0)
            seg_columns.append(column(seg_all[block][seq:seq + 1, :].astype(F32)))
        position.append(jnp.sum(count, axis=1, keepdims=True) - 1.0)
        seg_keys = jnp.concatenate(seg_columns, axis=0)
        seg_own = column(seg_ref[...][seq:seq + 1, :].astype(F32))
        seg_queries = jnp.sum(spread * seg_own, axis=0, keepdims=True)
        mask_tab[seq] = jnp.where(causal & (seg_keys == seg_queries), 0.0, -jnp.inf)
    half = (lane % (HD // 2)).astype(F32)
    freq = jnp.exp(half * (-2.0 * math.log(ROPE_BASE) / HD))
    angle = jnp.where(first, position[0], position[1]) * freq
    cos, sin = jnp.cos(angle), jnp.sin(angle)
    cos_swap, sin_swap = pltpu.roll(cos, HD // 2, 1), pltpu.roll(sin, HD // 2, 1)
    cos_tab[0] = jnp.where(first, cos, cos_swap)
    cos_tab[1] = jnp.where(first, cos_swap, cos)
    sin_tab[0] = jnp.where(first, -sin, sin_swap)
    sin_tab[1] = jnp.where(first, -sin_swap, sin)

    for index in range(2 * seqs, len(loads)):
        loads[index].wait()

    def query(chunk, _):
        seq, group = chunk // HK, chunk % HK
        raw = q_in[seq, :, wide(group)]
        c, s = cos_tab[seq, rows(me), :], sin_tab[seq, rows(me), :]
        for head in range(GROUP):
            piece = raw[:, head * HD:(head + 1) * HD].astype(F32)
            q_rot[chunk, head * toks:(head + 1) * toks, :] = rope(piece, c, s).astype(BF16)
        return 0

    lax.fori_loop(0, chunks, query, 0)

    def hand_on(chunk):
        def earlier(other, _):
            source = 2 * other + core
            for copy in kv_copy(source, me, 0, chunk, kv_send, kv_recv, False):
                copy.wait_recv()
            for copy in kv_copy(source, buddy, other, chunk, fw_send, fw_recv, True):
                copy.start()
            return 0

        lax.fori_loop(0, pair, earlier, 0)

    def take(chunk):
        def earlier(other, _):
            source = 2 * other + 1 - core
            for copy in kv_copy(source, me, 0, chunk, fw_send, fw_recv, False):
                copy.wait_recv()
            return 0

        lax.fori_loop(0, pair, earlier, 0)

        @pl.when(core == 1)
        def _():
            for copy in kv_copy(buddy, me, 0, chunk, kv_send, kv_recv, False):
                copy.wait_recv()

    def exchange(chunk, other, owner):
        return pltpu.make_async_remote_copy(
            part.at[chunk, owner], exch.at[chunk, other],
            ex_send.at[chunk, other], ex_recv.at[chunk, other],
            device_id=ctx_device(buddy), device_id_type=MESH)

    def cross(chunk, slot, other):
        return pltpu.make_async_remote_copy(
            sums.at[chunk, other], arrive.at[chunk, slot],
            cr_send.at[chunk, other], cr_recv.at[chunk, slot],
            device_id=ctx_device(2 * other + core), device_id_type=MESH)

    def pass_down(chunk):
        def earlier(other, _):
            exchange(chunk, other, 0).wait_recv()
            sums[chunk, other] = (part[chunk, 2 * other + core].astype(F32)
                                  + exch[chunk, other].astype(F32)).astype(BF16)
            cross(chunk, pair, other).start()
            return 0

        lax.fori_loop(0, pair, earlier, 0)

    bias_q[...] = jnp.zeros_like(bias_q)

    def attend(chunk, _):
        seq, group = chunk // HK, chunk % HK

        @pl.when(chunk + 1 < chunks)
        def _():
            hand_on(chunk + 1)

        take(chunk)
        keys = rope(k_all[seq, :, cols(group)].astype(F32), cos_tab[seq], sin_tab[seq]).astype(BF16)
        values = v_all[seq, :, cols(group)]
        queries, grads = q_rot[chunk], g_low[chunk]
        scores = lax.dot_general(keys, queries, NT, preferred_element_type=F32) + mask_tab[seq]
        top = jnp.max(scores, axis=0, keepdims=True)
        weights = jnp.exp((scores - top) * scale)
        probs = weights * (1.0 / jnp.sum(weights, axis=0, keepdims=True))
        grad_v = jnp.dot(probs.astype(BF16), grads, preferred_element_type=F32)
        grad_p = lax.dot_general(values, grads, NT, preferred_element_type=F32)
        grad_s = (probs * (grad_p - delta[chunk][0:1, :])).astype(BF16)
        grad_k = jnp.dot(grad_s, queries, preferred_element_type=F32) * scale
        grad_q = lax.dot_general(grad_s, keys, TN, preferred_element_type=F32) * scale
        for block in range(n):
            part[chunk, block, 0] = grad_k[block * toks:(block + 1) * toks].astype(BF16)
            part[chunk, block, 1] = grad_v[block * toks:(block + 1) * toks].astype(BF16)

            @pl.when(me == block)
            def _():
                own[chunk, 0] = grad_k[block * toks:(block + 1) * toks]
                own[chunk, 1] = grad_v[block * toks:(block + 1) * toks]

        def earlier(other, _):
            exchange(chunk, other, 2 * other + 1 - core).start()
            return 0

        lax.fori_loop(0, pair, earlier, 0)

        @pl.when(core == 1)
        def _():
            exchange(chunk, pair, buddy).start()

        c, s = cos_tab[seq, rows(me), :], sin_tab[seq, rows(me), :]
        totals, outs = [], []
        for head in range(GROUP):
            rounded = rope(grad_q[head * toks:(head + 1) * toks], c, -s).astype(BF16)
            outs.append(rounded)
            totals.append(jnp.sum(rounded.astype(F32), axis=0, keepdims=True))
        gq_out[chunk] = jnp.concatenate(outs, axis=1)
        bias_q[group] += jnp.concatenate(totals, axis=0)
        pltpu.make_async_copy(gq_out.at[chunk], gq_hbm.at[seq, :, wide(group)], out_sem.at[chunk]).start()

        @pl.when(chunk >= 1)
        def _():
            pass_down(chunk - 1)
        return 0

    hand_on(0)
    lax.fori_loop(0, chunks, attend, 0)
    pass_down(chunks - 1)

    bias_kv = [[jnp.zeros((1, HD), F32) for _ in range(HK)] for _ in range(2)]
    for chunk in range(chunks):
        seq, group = chunk // HK, chunk % HK

        @pl.when(core == 0)
        def _():
            exchange(chunk, pair, 0).wait_recv()
            own[chunk] += exch[chunk, pair].astype(F32)

        def incoming(other, _):
            cross(chunk, other, 0).wait_recv()
            own[chunk] += arrive[chunk, other].astype(F32)
            return 0

        lax.fori_loop(pair + 1, pairs, incoming, 0)
        c, s = cos_tab[seq, rows(me), :], sin_tab[seq, rows(me), :]
        key_grad = rope(own[chunk, 0], c, -s).astype(BF16)
        value_grad = own[chunk, 1].astype(BF16)
        gk_ref[seq, :, group * HD:(group + 1) * HD] = key_grad
        gv_ref[seq, :, group * HD:(group + 1) * HD] = value_grad
        bias_kv[0][group] += jnp.sum(key_grad.astype(F32), axis=0, keepdims=True)
        bias_kv[1][group] += jnp.sum(value_grad.astype(F32), axis=0, keepdims=True)
    heads_q = jnp.concatenate([bias_q[group] for group in range(HK)], axis=0)
    for shard in range(fsdps):
        lead = shard * HK // fsdps
        pieces = [heads_q[shard * q_rows:(shard + 1) * q_rows]]
        pieces += bias_kv[0][lead:lead + kv_rows] + bias_kv[1][lead:lead + kv_rows]
        pieces.append(jnp.zeros((bias_rows - q_rows - 2 * kv_rows, HD), F32))
        bias[shard] = jnp.concatenate(pieces, axis=0)

    def over_ctx(step, target):
        return pltpu.make_async_remote_copy(
            bias, bias_in.at[step], b1_send.at[step], b1_recv.at[step],
            device_id=ctx_device(target), device_id_type=MESH)

    for step in range(1, n):
        over_ctx(step, (me + step) % n).start()
    total = bias[...]
    for step in range(1, n):
        over_ctx(step, me).wait_recv()
        total = total + bias_in[step]
    bias_half[...] = total

    def over_rest(step):
        device = far_device(step)
        return pltpu.make_async_remote_copy(
            bias_half.at[device["fsdp"]], bias_half_in.at[step], b2_send.at[step], b2_recv.at[step],
            device_id=device, device_id_type=MESH)

    for step in range(1, others):
        over_rest(step).start()
    final = bias_half[fs]
    for step in range(1, others):
        over_rest(step).wait_recv()
        final = final + bias_half_in[step]
    bq_ref[...] = final[0:q_rows]
    bk_ref[...] = final[q_rows:q_rows + kv_rows]
    bv_ref[...] = final[q_rows + kv_rows:q_rows + 2 * kv_rows]

    def meta_end(target, _):
        for copy in meta_copy(me, target, target):
            copy.wait_send()
        return 0

    lax.fori_loop(me + 1, n, meta_end, 0)

    def end(chunk, _):
        def later(other, _):
            for copy in kv_copy(me, 2 * other + core, other, chunk, kv_send, kv_recv, False):
                copy.wait_send()
            return 0

        lax.fori_loop(pair + 1, pairs, later, 0)

        def earlier(other, _):
            for copy in kv_copy(2 * other + core, buddy, other, chunk, fw_send, fw_recv, True):
                copy.wait_send()
            exchange(chunk, other, 2 * other + 1 - core).wait_send()
            cross(chunk, pair, other).wait_send()
            return 0

        lax.fori_loop(0, pair, earlier, 0)

        @pl.when(core == 0)
        def _():
            for copy in kv_copy(me, buddy, pair, chunk, kv_send, kv_recv, False):
                copy.wait_send()

        @pl.when(core == 1)
        def _():
            exchange(chunk, pair, buddy).wait_send()

        pltpu.make_async_copy(
            gq_out.at[chunk], gq_hbm.at[chunk // HK, :, wide(chunk % HK)], out_sem.at[chunk]).wait()
        return 0

    lax.fori_loop(0, chunks, end, 0)
    for step in range(1, n):
        over_ctx(step, me).wait_send()
    for step in range(1, others):
        over_rest(step).wait_send()


def per_device(sizes, *args):
    n, reps, fsdps, seqs, toks = sizes
    length, pairs, chunks = n * toks, n // 2, seqs * HK
    rows, width, others = GROUP * toks, HQ * HD, reps * fsdps
    q_rows, kv_rows, bias_rows = bias_layout(fsdps)
    dma = pltpu.SemaphoreType.DMA
    vmem = pl.BlockSpec(memory_space=pltpu.VMEM)
    anywhere = pl.BlockSpec(memory_space=pl.ANY)
    out = pl.pallas_call(
        functools.partial(kernel, sizes),
        out_shape=(
            jax.ShapeDtypeStruct((seqs, toks, HQ * HD), BF16),
            jax.ShapeDtypeStruct((seqs, toks, HK * HD), BF16),
            jax.ShapeDtypeStruct((seqs, toks, HK * HD), BF16),
            jax.ShapeDtypeStruct((q_rows, HD), F32),
            jax.ShapeDtypeStruct((kv_rows, HD), F32),
            jax.ShapeDtypeStruct((kv_rows, HD), F32),
        ),
        in_specs=[anywhere] * 5 + [vmem] * 4,
        out_specs=(anywhere, vmem, vmem, vmem, vmem, vmem),
        scratch_shapes=[
            pltpu.VMEM((seqs, toks, width), BF16),
            pltpu.VMEM((seqs, toks, width), BF16),
            pltpu.VMEM((seqs, toks, width), BF16),
            pltpu.VMEM((seqs, length, HK * HD), BF16),
            pltpu.VMEM((seqs, length, HK * HD), BF16),
            pltpu.VMEM((n, seqs, toks), jnp.int32),
            pltpu.VMEM((n, seqs, toks), jnp.int32),
            pltpu.VMEM((chunks, rows, HD), BF16),
            pltpu.VMEM((chunks, rows, HD), BF16),
            pltpu.VMEM((chunks, 8, rows), F32),
            pltpu.VMEM((seqs, length, HD), F32),
            pltpu.VMEM((seqs, length, HD), F32),
            pltpu.VMEM((seqs, length, rows), F32),
            pltpu.VMEM((chunks, toks, GROUP * HD), BF16),
            pltpu.VMEM((chunks, n, 2, toks, HD), BF16),
            pltpu.VMEM((chunks, 2, toks, HD), F32),
            pltpu.VMEM((chunks, pairs, 2, toks, HD), BF16),
            pltpu.VMEM((chunks, pairs, 2, toks, HD), BF16),
            pltpu.VMEM((chunks, pairs, 2, toks, HD), BF16),
            pltpu.VMEM((HK, GROUP, HD), F32),
            pltpu.VMEM((fsdps, bias_rows, HD), F32),
            pltpu.VMEM((n, fsdps, bias_rows, HD), F32),
            pltpu.VMEM((fsdps, bias_rows, HD), F32),
            pltpu.VMEM((others, bias_rows, HD), F32),
            dma((5, seqs)),
            dma((chunks,)),
            dma((2, n)),
            dma((2, n)),
            dma((2, pairs, chunks)),
            dma((2, n, chunks)),
            dma((2, pairs, chunks)),
            dma((2, n, chunks)),
            dma((chunks, pairs)),
            dma((chunks, pairs)),
            dma((chunks, pairs)),
            dma((chunks, pairs)),
            dma((n,)),
            dma((n,)),
            dma((others,)),
            dma((others,)),
        ],
        compiler_params=pltpu.CompilerParams(
            collective_id=0, has_side_effects=True, vmem_limit_bytes=60 * 1024 * 1024
        ),
        name="attention_backward",
    )(*args)
    flat = [part.reshape(-1) for part in out[3:]]
    share = HK * HD // fsdps
    if share < HD:
        begin = (lax.axis_index("fsdp") * share) % HD
        flat[1:] = [lax.dynamic_slice(part, (begin,), (share,)) for part in flat[1:]]
    return out[:3] + tuple(flat)


def solution(mesh):
    tokens = P(("rep", "fsdp"), "ctx", None)
    flat = P(("rep", "fsdp"), "ctx")
    shape = dict(mesh.shape)

    def run(*args):
        n, reps, fsdps = shape["ctx"], shape["rep"], shape["fsdp"]
        sizes = (n, reps, fsdps, args[0].shape[0] // (reps * fsdps), args[0].shape[1] // n)
        return jax.shard_map(
            functools.partial(per_device, sizes),
            mesh=mesh,
            in_specs=(tokens,) * 5 + (flat,) * 4,
            out_specs=(tokens, tokens, tokens, P("fsdp"), P("fsdp"), P("fsdp")),
            check_vma=False,
        )(*args)

    return run
```

```python
import functools
import math

import jax
import jax.numpy as jnp
from jax import lax
from jax.experimental import pallas as pl
from jax.experimental.pallas import tpu as pltpu
from jax.sharding import PartitionSpec as P

HQ = 32
HK = 4
HD = 128
GROUP = HQ // HK
ROPE_BASE = 1000000.0
F32 = jnp.float32
BF16 = jnp.bfloat16
MESH = pl.DeviceIdType.MESH
NT = (((1,), (1,)), ((), ()))
TN = (((0,), (0,)), ((), ()))


def bias_layout(fsdps):
    q_rows, kv_rows = HQ // fsdps, max(1, HK // fsdps)
    return q_rows, kv_rows, -(-(q_rows + 2 * kv_rows) // 8) * 8


def rope(x, cos, sin):
    return x * cos + pltpu.roll(x, HD // 2, 1) * sin


def kernel(
    sizes,
    q_hbm, k_hbm, v_hbm, o_hbm, up_hbm, adv_ref, act_ref, seg_ref, code_ref,
    gq_hbm, gk_ref, gv_ref, bq_ref, bk_ref, bv_ref,
    q_in, o_in, up_in, k_all, v_all, code_all, seg_all,
    q_rot, g_low, delta, cos_tab, sin_tab, mask_tab,
    gq_out, part, own, exch, sums, arrive, bias_q, bias, bias_in, bias_half, bias_half_in,
    in_sem, out_sem, meta_send, meta_recv, kv_send, kv_recv, fw_send, fw_recv,
    ex_send, ex_recv, cr_send, cr_recv, b1_send, b1_recv, b2_send, b2_recv,
):
    n, reps, fsdps, seqs, toks = sizes
    length = n * toks
    pairs = n // 2
    chunks = seqs * HK
    width = GROUP * HD
    lanes = GROUP * toks
    scale = HD ** -0.5
    me = lax.axis_index("ctx")
    rep = lax.axis_index("rep")
    fs = lax.axis_index("fsdp")
    pair = me // 2
    core = me % 2
    buddy = me + 1 - 2 * core
    here = rep * fsdps + fs
    others = reps * fsdps
    q_rows, kv_rows, bias_rows = bias_layout(fsdps)

    def ctx_device(index):
        return {"ctx": index}

    def far_device(step):
        target = (here + step) % others
        return {"rep": target // fsdps, "fsdp": target % fsdps}

    def rows(index):
        return pl.ds(pl.multiple_of(index * toks, toks), toks)

    def cols(group):
        return pl.ds(pl.multiple_of(group * HD, HD), HD)

    def wide(group):
        return pl.ds(pl.multiple_of(group * width, width), width)

    loads = []
    for seq in range(seqs):
        loads.append(pltpu.make_async_copy(up_hbm.at[seq], up_in.at[seq], in_sem.at[0, seq]))
        loads.append(pltpu.make_async_copy(o_hbm.at[seq], o_in.at[seq], in_sem.at[1, seq]))
    for seq in range(seqs):
        loads.append(pltpu.make_async_copy(q_hbm.at[seq], q_in.at[seq], in_sem.at[2, seq]))
        loads.append(pltpu.make_async_copy(k_hbm.at[seq], k_all.at[seq, rows(me)], in_sem.at[3, seq]))
        loads.append(pltpu.make_async_copy(v_hbm.at[seq], v_all.at[seq, rows(me)], in_sem.at[4, seq]))
    for load in loads:
        load.start()

    barrier = pltpu.get_barrier_semaphore()
    for step in range(1, n):
        pl.semaphore_signal(barrier, inc=1, device_id=ctx_device((me + step) % n), device_id_type=MESH)
    for step in range(1, others):
        pl.semaphore_signal(barrier, inc=1, device_id=far_device(step), device_id_type=MESH)

    def clear(index, _):
        for seq in range(seqs):
            k_all[seq, rows(index), :] = jnp.zeros((toks, HK * HD), BF16)
            v_all[seq, rows(index), :] = jnp.zeros((toks, HK * HD), BF16)
        code_all[index] = jnp.zeros((seqs, toks), jnp.int32)
        seg_all[index] = jnp.zeros((seqs, toks), jnp.int32)
        return 0

    lax.fori_loop(me + 1, n, clear, 0)
    code_all[me] = code_ref[...]
    seg_all[me] = seg_ref[...]

    pl.semaphore_wait(barrier, n - 1 + others - 1)

    def meta_copy(source, target, slot):
        a = pltpu.make_async_remote_copy(
            code_ref, code_all.at[source], meta_send.at[0, slot], meta_recv.at[0, source],
            device_id=ctx_device(target), device_id_type=MESH)
        b = pltpu.make_async_remote_copy(
            seg_ref, seg_all.at[source], meta_send.at[1, slot], meta_recv.at[1, source],
            device_id=ctx_device(target), device_id_type=MESH)
        return a, b

    def meta_start(target, _):
        for copy in meta_copy(me, target, target):
            copy.start()
        return 0

    lax.fori_loop(me + 1, n, meta_start, 0)

    def kv_copy(source, target, slot, chunk, send, recv, forward):
        seq, group = chunk // HK, chunk % HK
        made = []
        for kind, (hbm, held) in enumerate(((k_hbm, k_all), (v_hbm, v_all))):
            place = held.at[seq, rows(source), cols(group)]
            origin = place if forward else hbm.at[seq, :, cols(group)]
            made.append(pltpu.make_async_remote_copy(
                origin, place, send.at[kind, slot, chunk], recv.at[kind, source, chunk],
                device_id=ctx_device(target), device_id_type=MESH))
        return made

    def kv_start(chunk, _):
        def later(other, _):
            for copy in kv_copy(me, 2 * other + core, other, chunk, kv_send, kv_recv, False):
                copy.start()
            return 0

        lax.fori_loop(pair + 1, pairs, later, 0)

        @pl.when(core == 0)
        def _():
            for copy in kv_copy(me, buddy, pair, chunk, kv_send, kv_recv, False):
                copy.start()
        return 0

    lax.fori_loop(0, chunks, kv_start, 0)

    eye = lax.broadcasted_iota(jnp.int32, (toks, toks), 0) == lax.broadcasted_iota(
        jnp.int32, (toks, toks), 1)

    def column(row):
        return jnp.sum(jnp.where(eye, row, 0.0), axis=1, keepdims=True)

    weight_rows = adv_ref[...] * act_ref[...].astype(F32)
    ones = jnp.ones((8, HD), BF16)
    for seq in range(seqs):
        weight = column(weight_rows[seq:seq + 1, :])
        loads[2 * seq].wait()
        loads[2 * seq + 1].wait()

        def cotangent(group, _, seq=seq, weight=weight):
            chunk = seq * HK + group
            up = up_in[seq, :, wide(group)]
            out = o_in[seq, :, wide(group)]
            high, low = [], []
            for head in range(GROUP):
                part_cols = slice(head * HD, (head + 1) * HD)
                rounded = (weight * up[:, part_cols].astype(F32)).astype(BF16)
                g_low[chunk, head * toks:(head + 1) * toks, :] = rounded
                product = rounded.astype(F32) * out[:, part_cols].astype(F32)
                top = product.astype(BF16)
                high.append(top)
                low.append((product - top.astype(F32)).astype(BF16))
            total = lax.dot_general(ones, jnp.concatenate(high, axis=0), NT, preferred_element_type=F32)
            total += lax.dot_general(ones, jnp.concatenate(low, axis=0), NT, preferred_element_type=F32)
            delta[chunk] = total
            return 0

        lax.fori_loop(0, HK, cotangent, 0)

    def meta_wait(source, _):
        for copy in meta_copy(source, me, 0):
            copy.wait_recv()
        return 0

    lax.fori_loop(0, me, meta_wait, 0)
    row_of = lax.broadcasted_iota(jnp.int32, (length, toks), 0)
    col_of = lax.broadcasted_iota(jnp.int32, (length, toks), 1)
    lane = lax.broadcasted_iota(jnp.int32, (1, HD), 1)
    first = lane < HD // 2
    key_index = lax.broadcasted_iota(jnp.int32, (length, lanes), 0)
    query_index = lax.broadcasted_iota(jnp.int32, (length, lanes), 1) % toks + me * toks
    causal = key_index <= query_index
    spread = (lax.broadcasted_iota(jnp.int32, (toks, lanes), 0)
              == lax.broadcasted_iota(jnp.int32, (toks, lanes), 1) % toks).astype(F32)
    position = []
    for seq in range(seqs):
        count = jnp.zeros((length, toks), F32)
        seg_columns = []
        for block in range(n):
            starts = jnp.where(code_all[block][seq:seq + 1, :] <= 1, 1.0, 0.0)
            count = count + jnp.where(col_of + block * toks <= row_of, starts, 0.0)
            seg_columns.append(column(seg_all[block][seq:seq + 1, :].astype(F32)))
        position.append(jnp.sum(count, axis=1, keepdims=True) - 1.0)
        seg_keys = jnp.concatenate(seg_columns, axis=0)
        seg_own = column(seg_ref[...][seq:seq + 1, :].astype(F32))
        seg_queries = jnp.sum(spread * seg_own, axis=0, keepdims=True)
        mask_tab[seq] = jnp.where(causal & (seg_keys == seg_queries), 0.0, -jnp.inf)
    half = (lane % (HD // 2)).astype(F32)
    freq = jnp.exp(half * (-2.0 * math.log(ROPE_BASE) / HD))
    angle = jnp.where(first, position[0], position[1]) * freq
    cos, sin = jnp.cos(angle), jnp.sin(angle)
    cos_swap, sin_swap = pltpu.roll(cos, HD // 2, 1), pltpu.roll(sin, HD // 2, 1)
    cos_tab[0] = jnp.where(first, cos, cos_swap)
    cos_tab[1] = jnp.where(first, cos_swap, cos)
    sin_tab[0] = jnp.where(first, -sin, sin_swap)
    sin_tab[1] = jnp.where(first, -sin_swap, sin)

    for index in range(2 * seqs, len(loads)):
        loads[index].wait()

    def query(chunk, _):
        seq, group = chunk // HK, chunk % HK
        raw = q_in[seq, :, wide(group)]
        c, s = cos_tab[seq, rows(me), :], sin_tab[seq, rows(me), :]
        for head in range(GROUP):
            piece = raw[:, head * HD:(head + 1) * HD].astype(F32)
            q_rot[chunk, head * toks:(head + 1) * toks, :] = rope(piece, c, s).astype(BF16)
        return 0

    lax.fori_loop(0, chunks, query, 0)

    def hand_on(chunk):
        def earlier(other, _):
            source = 2 * other + core
            for copy in kv_copy(source, me, 0, chunk, kv_send, kv_recv, False):
                copy.wait_recv()
            for copy in kv_copy(source, buddy, other, chunk, fw_send, fw_recv, True):
                copy.start()
            return 0

        lax.fori_loop(0, pair, earlier, 0)

    def take(chunk):
        def earlier(other, _):
            source = 2 * other + 1 - core
            for copy in kv_copy(source, me, 0, chunk, fw_send, fw_recv, False):
                copy.wait_recv()
            return 0

        lax.fori_loop(0, pair, earlier, 0)

        @pl.when(core == 1)
        def _():
            for copy in kv_copy(buddy, me, 0, chunk, kv_send, kv_recv, False):
                copy.wait_recv()

    def exchange(chunk, other, owner):
        return pltpu.make_async_remote_copy(
            part.at[chunk, owner], exch.at[chunk, other],
            ex_send.at[chunk, other], ex_recv.at[chunk, other],
            device_id=ctx_device(buddy), device_id_type=MESH)

    def cross(chunk, slot, other):
        return pltpu.make_async_remote_copy(
            sums.at[chunk, other], arrive.at[chunk, slot],
            cr_send.at[chunk, other], cr_recv.at[chunk, slot],
            device_id=ctx_device(2 * other + core), device_id_type=MESH)

    def pass_down(chunk):
        def earlier(other, _):
            exchange(chunk, other, 0).wait_recv()
            sums[chunk, other] = (part[chunk, 2 * other + core].astype(F32)
                                  + exch[chunk, other].astype(F32)).astype(BF16)
            cross(chunk, pair, other).start()
            return 0

        lax.fori_loop(0, pair, earlier, 0)

    bias_q[...] = jnp.zeros_like(bias_q)

    def attend(chunk, _):
        seq, group = chunk // HK, chunk % HK

        @pl.when(chunk + 1 < chunks)
        def _():
            hand_on(chunk + 1)

        take(chunk)
        keys = rope(k_all[seq, :, cols(group)].astype(F32), cos_tab[seq], sin_tab[seq]).astype(BF16)
        values = v_all[seq, :, cols(group)]
        queries, grads = q_rot[chunk], g_low[chunk]
        scores = lax.dot_general(keys, queries, NT, preferred_element_type=F32) + mask_tab[seq]
        top = jnp.max(scores, axis=0, keepdims=True)
        weights = jnp.exp((scores - top) * scale)
        probs = weights * (1.0 / jnp.sum(weights, axis=0, keepdims=True))
        grad_v = jnp.dot(probs.astype(BF16), grads, preferred_element_type=F32)
        grad_p = lax.dot_general(values, grads, NT, preferred_element_type=F32)
        grad_s = (probs * (grad_p - delta[chunk][0:1, :])).astype(BF16)
        grad_k = jnp.dot(grad_s, queries, preferred_element_type=F32) * scale
        grad_q = lax.dot_general(grad_s, keys, TN, preferred_element_type=F32) * scale
        for block in range(n):
            part[chunk, block, 0] = grad_k[block * toks:(block + 1) * toks].astype(BF16)
            part[chunk, block, 1] = grad_v[block * toks:(block + 1) * toks].astype(BF16)

            @pl.when(me == block)
            def _():
                own[chunk, 0] = grad_k[block * toks:(block + 1) * toks]
                own[chunk, 1] = grad_v[block * toks:(block + 1) * toks]

        def earlier(other, _):
            exchange(chunk, other, 2 * other + 1 - core).start()
            return 0

        lax.fori_loop(0, pair, earlier, 0)

        @pl.when(core == 1)
        def _():
            exchange(chunk, pair, buddy).start()

        c, s = cos_tab[seq, rows(me), :], sin_tab[seq, rows(me), :]
        totals, outs = [], []
        for head in range(GROUP):
            rounded = rope(grad_q[head * toks:(head + 1) * toks], c, -s).astype(BF16)
            outs.append(rounded)
            totals.append(jnp.sum(rounded.astype(F32), axis=0, keepdims=True))
        gq_out[chunk] = jnp.concatenate(outs, axis=1)
        bias_q[group] += jnp.concatenate(totals, axis=0)
        pltpu.make_async_copy(gq_out.at[chunk], gq_hbm.at[seq, :, wide(group)], out_sem.at[chunk]).start()

        @pl.when(chunk >= 1)
        def _():
            pass_down(chunk - 1)
        return 0

    hand_on(0)
    lax.fori_loop(0, chunks, attend, 0)
    pass_down(chunks - 1)

    bias_kv = [[jnp.zeros((1, HD), F32) for _ in range(HK)] for _ in range(2)]
    for chunk in range(chunks):
        seq, group = chunk // HK, chunk % HK

        @pl.when(core == 0)
        def _():
            exchange(chunk, pair, 0).wait_recv()
            own[chunk] += exch[chunk, pair].astype(F32)

        def incoming(other, _):
            cross(chunk, other, 0).wait_recv()
            own[chunk] += arrive[chunk, other].astype(F32)
            return 0

        lax.fori_loop(pair + 1, pairs, incoming, 0)
        c, s = cos_tab[seq, rows(me), :], sin_tab[seq, rows(me), :]
        key_grad = rope(own[chunk, 0], c, -s).astype(BF16)
        value_grad = own[chunk, 1].astype(BF16)
        gk_ref[seq, :, group * HD:(group + 1) * HD] = key_grad
        gv_ref[seq, :, group * HD:(group + 1) * HD] = value_grad
        bias_kv[0][group] += jnp.sum(key_grad.astype(F32), axis=0, keepdims=True)
        bias_kv[1][group] += jnp.sum(value_grad.astype(F32), axis=0, keepdims=True)
    heads_q = jnp.concatenate([bias_q[group] for group in range(HK)], axis=0)
    for shard in range(fsdps):
        lead = shard * HK // fsdps
        pieces = [heads_q[shard * q_rows:(shard + 1) * q_rows]]
        pieces += bias_kv[0][lead:lead + kv_rows] + bias_kv[1][lead:lead + kv_rows]
        pieces.append(jnp.zeros((bias_rows - q_rows - 2 * kv_rows, HD), F32))
        bias[shard] = jnp.concatenate(pieces, axis=0)

    def over_ctx(step, target):
        return pltpu.make_async_remote_copy(
            bias, bias_in.at[step], b1_send.at[step], b1_recv.at[step],
            device_id=ctx_device(target), device_id_type=MESH)

    for step in range(1, n):
        over_ctx(step, (me + step) % n).start()
    total = bias[...]
    for step in range(1, n):
        over_ctx(step, me).wait_recv()
        total = total + bias_in[step]
    bias_half[...] = total

    def over_rest(step):
        device = far_device(step)
        return pltpu.make_async_remote_copy(
            bias_half.at[device["fsdp"]], bias_half_in.at[step], b2_send.at[step], b2_recv.at[step],
            device_id=device, device_id_type=MESH)

    for step in range(1, others):
        over_rest(step).start()
    final = bias_half[fs]
    for step in range(1, others):
        over_rest(step).wait_recv()
        final = final + bias_half_in[step]
    bq_ref[...] = final[0:q_rows]
    bk_ref[...] = final[q_rows:q_rows + kv_rows]
    bv_ref[...] = final[q_rows + kv_rows:q_rows + 2 * kv_rows]

    def meta_end(target, _):
        for copy in meta_copy(me, target, target):
            copy.wait_send()
        return 0

    lax.fori_loop(me + 1, n, meta_end, 0)

    def end(chunk, _):
        def later(other, _):
            for copy in kv_copy(me, 2 * other + core, other, chunk, kv_send, kv_recv, False):
                copy.wait_send()
            return 0

        lax.fori_loop(pair + 1, pairs, later, 0)

        def earlier(other, _):
            for copy in kv_copy(2 * other + core, buddy, other, chunk, fw_send, fw_recv, True):
                copy.wait_send()
            exchange(chunk, other, 2 * other + 1 - core).wait_send()
            cross(chunk, pair, other).wait_send()
            return 0

        lax.fori_loop(0, pair, earlier, 0)

        @pl.when(core == 0)
        def _():
            for copy in kv_copy(me, buddy, pair, chunk, kv_send, kv_recv, False):
                copy.wait_send()

        @pl.when(core == 1)
        def _():
            exchange(chunk, pair, buddy).wait_send()

        pltpu.make_async_copy(
            gq_out.at[chunk], gq_hbm.at[chunk // HK, :, wide(chunk % HK)], out_sem.at[chunk]).wait()
        return 0

    lax.fori_loop(0, chunks, end, 0)
    for step in range(1, n):
        over_ctx(step, me).wait_send()
    for step in range(1, others):
        over_rest(step).wait_send()


PIECES = 4


def finish(*refs):
    made, wide_hbm = refs[:6], refs[6]
    held, load_sem, store_sem = refs[12:]
    results = refs[6:12]
    seqs = made[0].shape[0]
    span = made[0].shape[2] // PIECES
    loads, stores = [], []
    for piece in range(seqs * PIECES):
        place = (piece // PIECES, slice(None), pl.ds(piece % PIECES * span, span))
        loads.append(pltpu.make_async_copy(made[0].at[place], held.at[piece], load_sem.at[piece]))
        stores.append(pltpu.make_async_copy(held.at[piece], wide_hbm.at[place], store_sem.at[piece]))
    for load in loads:
        load.start()
    for source, result in zip(made[1:], results[1:]):
        result[...] = source[...]
    for load, store in zip(loads, stores):
        load.wait()
        store.start()
    for store in stores:
        store.wait()


def per_device(sizes, *args):
    n, reps, fsdps, seqs, toks = sizes
    length, pairs, chunks = n * toks, n // 2, seqs * HK
    rows, width, others = GROUP * toks, HQ * HD, reps * fsdps
    q_rows, kv_rows, bias_rows = bias_layout(fsdps)
    dma = pltpu.SemaphoreType.DMA
    vmem = pl.BlockSpec(memory_space=pltpu.VMEM)
    anywhere = pl.BlockSpec(memory_space=pl.ANY)
    out = pl.pallas_call(
        functools.partial(kernel, sizes),
        out_shape=(
            jax.ShapeDtypeStruct((seqs, toks, HQ * HD), BF16),
            jax.ShapeDtypeStruct((seqs, toks, HK * HD), BF16),
            jax.ShapeDtypeStruct((seqs, toks, HK * HD), BF16),
            jax.ShapeDtypeStruct((q_rows, HD), F32),
            jax.ShapeDtypeStruct((kv_rows, HD), F32),
            jax.ShapeDtypeStruct((kv_rows, HD), F32),
        ),
        in_specs=[anywhere] * 5 + [vmem] * 4,
        out_specs=(anywhere, vmem, vmem, vmem, vmem, vmem),
        scratch_shapes=[
            pltpu.VMEM((seqs, toks, width), BF16),
            pltpu.VMEM((seqs, toks, width), BF16),
            pltpu.VMEM((seqs, toks, width), BF16),
            pltpu.VMEM((seqs, length, HK * HD), BF16),
            pltpu.VMEM((seqs, length, HK * HD), BF16),
            pltpu.VMEM((n, seqs, toks), jnp.int32),
            pltpu.VMEM((n, seqs, toks), jnp.int32),
            pltpu.VMEM((chunks, rows, HD), BF16),
            pltpu.VMEM((chunks, rows, HD), BF16),
            pltpu.VMEM((chunks, 8, rows), F32),
            pltpu.VMEM((seqs, length, HD), F32),
            pltpu.VMEM((seqs, length, HD), F32),
            pltpu.VMEM((seqs, length, rows), F32),
            pltpu.VMEM((chunks, toks, GROUP * HD), BF16),
            pltpu.VMEM((chunks, n, 2, toks, HD), BF16),
            pltpu.VMEM((chunks, 2, toks, HD), F32),
            pltpu.VMEM((chunks, pairs, 2, toks, HD), BF16),
            pltpu.VMEM((chunks, pairs, 2, toks, HD), BF16),
            pltpu.VMEM((chunks, pairs, 2, toks, HD), BF16),
            pltpu.VMEM((HK, GROUP, HD), F32),
            pltpu.VMEM((fsdps, bias_rows, HD), F32),
            pltpu.VMEM((n, fsdps, bias_rows, HD), F32),
            pltpu.VMEM((fsdps, bias_rows, HD), F32),
            pltpu.VMEM((others, bias_rows, HD), F32),
            dma((5, seqs)),
            dma((chunks,)),
            dma((2, n)),
            dma((2, n)),
            dma((2, pairs, chunks)),
            dma((2, n, chunks)),
            dma((2, pairs, chunks)),
            dma((2, n, chunks)),
            dma((chunks, pairs)),
            dma((chunks, pairs)),
            dma((chunks, pairs)),
            dma((chunks, pairs)),
            dma((n,)),
            dma((n,)),
            dma((others,)),
            dma((others,)),
        ],
        compiler_params=pltpu.CompilerParams(
            collective_id=0, has_side_effects=True, vmem_limit_bytes=60 * 1024 * 1024
        ),
        name="attention_backward",
    )(*args)
    out = pl.pallas_call(
        finish,
        out_shape=tuple(jax.ShapeDtypeStruct(part.shape, part.dtype) for part in out),
        in_specs=[anywhere] + [vmem] * 5,
        out_specs=(anywhere,) + (vmem,) * 5,
        scratch_shapes=[
            pltpu.VMEM((seqs * PIECES, toks, width // PIECES), BF16),
            dma((seqs * PIECES,)),
            dma((seqs * PIECES,)),
        ],
        name="finish",
    )(*out)
    flat = [part.reshape(-1) for part in out[3:]]
    share = HK * HD // fsdps
    if share < HD:
        begin = (lax.axis_index("fsdp") * share) % HD
        flat[1:] = [lax.dynamic_slice(part, (begin,), (share,)) for part in flat[1:]]
    return out[:3] + tuple(flat)


def solution(mesh):
    tokens = P(("rep", "fsdp"), "ctx", None)
    flat = P(("rep", "fsdp"), "ctx")
    shape = dict(mesh.shape)

    def run(*args):
        n, reps, fsdps = shape["ctx"], shape["rep"], shape["fsdp"]
        sizes = (n, reps, fsdps, args[0].shape[0] // (reps * fsdps), args[0].shape[1] // n)
        return jax.shard_map(
            functools.partial(per_device, sizes),
            mesh=mesh,
            in_specs=(tokens,) * 5 + (flat,) * 4,
            out_specs=(tokens, tokens, tokens, P("fsdp"), P("fsdp"), P("fsdp")),
            check_vma=False,
        )(*args)

    return run
```

```python
import functools
import math

import jax
import jax.numpy as jnp
from jax import lax
from jax.experimental import pallas as pl
from jax.experimental.pallas import tpu as pltpu
from jax.sharding import PartitionSpec as P

HQ = 32
HK = 4
HD = 128
GROUP = HQ // HK
ROPE_BASE = 1000000.0
F32 = jnp.float32
BF16 = jnp.bfloat16
MESH = pl.DeviceIdType.MESH
NT = (((1,), (1,)), ((), ()))
TN = (((0,), (0,)), ((), ()))


def bias_layout(fsdps):
    q_rows, kv_rows = HQ // fsdps, max(1, HK // fsdps)
    return q_rows, kv_rows, -(-(q_rows + 2 * kv_rows) // 8) * 8


def rope(x, cos, sin):
    return x * cos + pltpu.roll(x, HD // 2, 1) * sin


def kernel(
    sizes,
    q_hbm, k_hbm, v_hbm, o_hbm, up_hbm, adv_ref, act_ref, seg_ref, code_ref,
    gq_hbm, gk_ref, gv_ref, bq_ref, bk_ref, bv_ref,
    q_in, o_in, up_in, k_all, v_all, code_all, seg_all,
    q_rot, g_low, delta, cos_tab, sin_tab, mask_tab,
    gq_out, part, own, exch, sums, arrive, bias_q, bias, bias_in, bias_half, bias_half_in,
    in_sem, out_sem, meta_send, meta_recv, kv_send, kv_recv, fw_send, fw_recv,
    ex_send, ex_recv, cr_send, cr_recv, b1_send, b1_recv, b2_send, b2_recv,
):
    n, reps, fsdps, seqs, toks = sizes
    length = n * toks
    pairs = n // 2
    chunks = seqs * HK
    width = GROUP * HD
    lanes = GROUP * toks
    scale = HD ** -0.5
    me = lax.axis_index("ctx")
    rep = lax.axis_index("rep")
    fs = lax.axis_index("fsdp")
    pair = me // 2
    core = me % 2
    buddy = me + 1 - 2 * core
    here = rep * fsdps + fs
    others = reps * fsdps
    q_rows, kv_rows, bias_rows = bias_layout(fsdps)

    def ctx_device(index):
        return {"ctx": index}

    def far_device(step):
        target = (here + step) % others
        return {"rep": target // fsdps, "fsdp": target % fsdps}

    def rows(index):
        return pl.ds(pl.multiple_of(index * toks, toks), toks)

    def cols(group):
        return pl.ds(pl.multiple_of(group * HD, HD), HD)

    def wide(group):
        return pl.ds(pl.multiple_of(group * width, width), width)

    loads = []
    for seq in range(seqs):
        loads.append(pltpu.make_async_copy(up_hbm.at[seq], up_in.at[seq], in_sem.at[0, seq]))
        loads.append(pltpu.make_async_copy(o_hbm.at[seq], o_in.at[seq], in_sem.at[1, seq]))
    for seq in range(seqs):
        loads.append(pltpu.make_async_copy(q_hbm.at[seq], q_in.at[seq], in_sem.at[2, seq]))
        loads.append(pltpu.make_async_copy(k_hbm.at[seq], k_all.at[seq, rows(me)], in_sem.at[3, seq]))
        loads.append(pltpu.make_async_copy(v_hbm.at[seq], v_all.at[seq, rows(me)], in_sem.at[4, seq]))
    for load in loads:
        load.start()

    barrier = pltpu.get_barrier_semaphore()
    for step in range(1, n):
        pl.semaphore_signal(barrier, inc=1, device_id=ctx_device((me + step) % n), device_id_type=MESH)
    for step in range(1, others):
        pl.semaphore_signal(barrier, inc=1, device_id=far_device(step), device_id_type=MESH)

    def clear(index, _):
        for seq in range(seqs):
            k_all[seq, rows(index), :] = jnp.zeros((toks, HK * HD), BF16)
            v_all[seq, rows(index), :] = jnp.zeros((toks, HK * HD), BF16)
        code_all[index] = jnp.zeros((seqs, toks), jnp.int32)
        seg_all[index] = jnp.zeros((seqs, toks), jnp.int32)
        return 0

    lax.fori_loop(me + 1, n, clear, 0)
    code_all[me] = code_ref[...]
    seg_all[me] = seg_ref[...]

    pl.semaphore_wait(barrier, n - 1 + others - 1)

    def meta_copy(source, target, slot):
        a = pltpu.make_async_remote_copy(
            code_ref, code_all.at[source], meta_send.at[0, slot], meta_recv.at[0, source],
            device_id=ctx_device(target), device_id_type=MESH)
        b = pltpu.make_async_remote_copy(
            seg_ref, seg_all.at[source], meta_send.at[1, slot], meta_recv.at[1, source],
            device_id=ctx_device(target), device_id_type=MESH)
        return a, b

    def meta_start(target, _):
        for copy in meta_copy(me, target, target):
            copy.start()
        return 0

    lax.fori_loop(me + 1, n, meta_start, 0)

    def kv_copy(source, target, slot, chunk, send, recv, forward):
        seq, group = chunk // HK, chunk % HK
        made = []
        for kind, (hbm, held) in enumerate(((k_hbm, k_all), (v_hbm, v_all))):
            place = held.at[seq, rows(source), cols(group)]
            origin = place if forward else hbm.at[seq, :, cols(group)]
            made.append(pltpu.make_async_remote_copy(
                origin, place, send.at[kind, slot, chunk], recv.at[kind, source, chunk],
                device_id=ctx_device(target), device_id_type=MESH))
        return made

    def kv_start(chunk, _):
        def later(other, _):
            for copy in kv_copy(me, 2 * other + core, other, chunk, kv_send, kv_recv, False):
                copy.start()
            return 0

        lax.fori_loop(pair + 1, pairs, later, 0)

        @pl.when(core == 0)
        def _():
            for copy in kv_copy(me, buddy, pair, chunk, kv_send, kv_recv, False):
                copy.start()
        return 0

    lax.fori_loop(0, chunks, kv_start, 0)

    eye = lax.broadcasted_iota(jnp.int32, (toks, toks), 0) == lax.broadcasted_iota(
        jnp.int32, (toks, toks), 1)

    def column(row):
        return jnp.sum(jnp.where(eye, row, 0.0), axis=1, keepdims=True)

    weight_rows = adv_ref[...] * act_ref[...].astype(F32)
    ones = jnp.ones((8, HD), BF16)
    for seq in range(seqs):
        weight = column(weight_rows[seq:seq + 1, :])
        loads[2 * seq].wait()
        loads[2 * seq + 1].wait()

        def cotangent(group, _, seq=seq, weight=weight):
            chunk = seq * HK + group
            up = up_in[seq, :, wide(group)]
            out = o_in[seq, :, wide(group)]
            high, low = [], []
            for head in range(GROUP):
                part_cols = slice(head * HD, (head + 1) * HD)
                rounded = (weight * up[:, part_cols].astype(F32)).astype(BF16)
                g_low[chunk, head * toks:(head + 1) * toks, :] = rounded
                product = rounded.astype(F32) * out[:, part_cols].astype(F32)
                top = product.astype(BF16)
                high.append(top)
                low.append((product - top.astype(F32)).astype(BF16))
            total = lax.dot_general(ones, jnp.concatenate(high, axis=0), NT, preferred_element_type=F32)
            total += lax.dot_general(ones, jnp.concatenate(low, axis=0), NT, preferred_element_type=F32)
            delta[chunk] = total
            return 0

        lax.fori_loop(0, HK, cotangent, 0)

    def meta_wait(source, _):
        for copy in meta_copy(source, me, 0):
            copy.wait_recv()
        return 0

    lax.fori_loop(0, me, meta_wait, 0)
    row_of = lax.broadcasted_iota(jnp.int32, (length, toks), 0)
    col_of = lax.broadcasted_iota(jnp.int32, (length, toks), 1)
    lane = lax.broadcasted_iota(jnp.int32, (1, HD), 1)
    first = lane < HD // 2
    key_index = lax.broadcasted_iota(jnp.int32, (length, lanes), 0)
    query_index = lax.broadcasted_iota(jnp.int32, (length, lanes), 1) % toks + me * toks
    causal = key_index <= query_index
    spread = (lax.broadcasted_iota(jnp.int32, (toks, lanes), 0)
              == lax.broadcasted_iota(jnp.int32, (toks, lanes), 1) % toks).astype(F32)
    position = []
    for seq in range(seqs):
        count = jnp.zeros((length, toks), F32)
        seg_columns = []
        for block in range(n):
            starts = jnp.where(code_all[block][seq:seq + 1, :] <= 1, 1.0, 0.0)
            count = count + jnp.where(col_of + block * toks <= row_of, starts, 0.0)
            seg_columns.append(column(seg_all[block][seq:seq + 1, :].astype(F32)))
        position.append(jnp.sum(count, axis=1, keepdims=True) - 1.0)
        seg_keys = jnp.concatenate(seg_columns, axis=0)
        seg_own = column(seg_ref[...][seq:seq + 1, :].astype(F32))
        seg_queries = jnp.sum(spread * seg_own, axis=0, keepdims=True)
        mask_tab[seq] = jnp.where(causal & (seg_keys == seg_queries), 0.0, -jnp.inf)
    half = (lane % (HD // 2)).astype(F32)
    freq = jnp.exp(half * (-2.0 * math.log(ROPE_BASE) / HD))
    angle = jnp.where(first, position[0], position[1]) * freq
    cos, sin = jnp.cos(angle), jnp.sin(angle)
    cos_swap, sin_swap = pltpu.roll(cos, HD // 2, 1), pltpu.roll(sin, HD // 2, 1)
    cos_tab[0] = jnp.where(first, cos, cos_swap)
    cos_tab[1] = jnp.where(first, cos_swap, cos)
    sin_tab[0] = jnp.where(first, -sin, sin_swap)
    sin_tab[1] = jnp.where(first, -sin_swap, sin)

    for index in range(2 * seqs, len(loads)):
        loads[index].wait()

    def query(chunk, _):
        seq, group = chunk // HK, chunk % HK
        raw = q_in[seq, :, wide(group)]
        c, s = cos_tab[seq, rows(me), :], sin_tab[seq, rows(me), :]
        for head in range(GROUP):
            piece = raw[:, head * HD:(head + 1) * HD].astype(F32)
            q_rot[chunk, head * toks:(head + 1) * toks, :] = rope(piece, c, s).astype(BF16)
        return 0

    lax.fori_loop(0, chunks, query, 0)

    def hand_on(chunk):
        def earlier(other, _):
            source = 2 * other + core
            for copy in kv_copy(source, me, 0, chunk, kv_send, kv_recv, False):
                copy.wait_recv()
            for copy in kv_copy(source, buddy, other, chunk, fw_send, fw_recv, True):
                copy.start()
            return 0

        lax.fori_loop(0, pair, earlier, 0)

    def take(chunk):
        def earlier(other, _):
            source = 2 * other + 1 - core
            for copy in kv_copy(source, me, 0, chunk, fw_send, fw_recv, False):
                copy.wait_recv()
            return 0

        lax.fori_loop(0, pair, earlier, 0)

        @pl.when(core == 1)
        def _():
            for copy in kv_copy(buddy, me, 0, chunk, kv_send, kv_recv, False):
                copy.wait_recv()

    def exchange(chunk, other, owner):
        return pltpu.make_async_remote_copy(
            part.at[chunk, owner], exch.at[chunk, other],
            ex_send.at[chunk, other], ex_recv.at[chunk, other],
            device_id=ctx_device(buddy), device_id_type=MESH)

    def cross(chunk, slot, other):
        return pltpu.make_async_remote_copy(
            sums.at[chunk, other], arrive.at[chunk, slot],
            cr_send.at[chunk, other], cr_recv.at[chunk, slot],
            device_id=ctx_device(2 * other + core), device_id_type=MESH)

    def pass_down(chunk):
        def earlier(other, _):
            exchange(chunk, other, 0).wait_recv()
            sums[chunk, other] = (part[chunk, 2 * other + core].astype(F32)
                                  + exch[chunk, other].astype(F32)).astype(BF16)
            cross(chunk, pair, other).start()
            return 0

        lax.fori_loop(0, pair, earlier, 0)

    bias_q[...] = jnp.zeros_like(bias_q)

    def attend(chunk, _):
        seq, group = chunk // HK, chunk % HK

        @pl.when(chunk + 1 < chunks)
        def _():
            hand_on(chunk + 1)

        take(chunk)
        keys = rope(k_all[seq, :, cols(group)].astype(F32), cos_tab[seq], sin_tab[seq]).astype(BF16)
        values = v_all[seq, :, cols(group)]
        queries, grads = q_rot[chunk], g_low[chunk]
        scores = lax.dot_general(keys, queries, NT, preferred_element_type=F32) + mask_tab[seq]
        top = jnp.max(scores, axis=0, keepdims=True)
        weights = jnp.exp((scores - top) * scale)
        probs = weights * (1.0 / jnp.sum(weights, axis=0, keepdims=True))
        grad_v = jnp.dot(probs.astype(BF16), grads, preferred_element_type=F32)
        grad_p = lax.dot_general(values, grads, NT, preferred_element_type=F32)
        grad_s = (probs * (grad_p - delta[chunk][0:1, :])).astype(BF16)
        grad_k = jnp.dot(grad_s, queries, preferred_element_type=F32) * scale
        grad_q = lax.dot_general(grad_s, keys, TN, preferred_element_type=F32) * scale
        for block in range(n):
            part[chunk, block, 0] = grad_k[block * toks:(block + 1) * toks].astype(BF16)
            part[chunk, block, 1] = grad_v[block * toks:(block + 1) * toks].astype(BF16)

            @pl.when(me == block)
            def _():
                own[chunk, 0] = grad_k[block * toks:(block + 1) * toks]
                own[chunk, 1] = grad_v[block * toks:(block + 1) * toks]

        def earlier(other, _):
            exchange(chunk, other, 2 * other + 1 - core).start()
            return 0

        lax.fori_loop(0, pair, earlier, 0)

        @pl.when(core == 1)
        def _():
            exchange(chunk, pair, buddy).start()

        c, s = cos_tab[seq, rows(me), :], sin_tab[seq, rows(me), :]
        totals, outs = [], []
        for head in range(GROUP):
            rounded = rope(grad_q[head * toks:(head + 1) * toks], c, -s).astype(BF16)
            outs.append(rounded)
            totals.append(jnp.sum(rounded.astype(F32), axis=0, keepdims=True))
        gq_out[chunk] = jnp.concatenate(outs, axis=1)
        bias_q[group] += jnp.concatenate(totals, axis=0)
        pltpu.make_async_copy(gq_out.at[chunk], gq_hbm.at[seq, :, wide(group)], out_sem.at[chunk]).start()

        @pl.when(chunk >= 1)
        def _():
            pass_down(chunk - 1)
        return 0

    hand_on(0)
    lax.fori_loop(0, chunks, attend, 0, unroll=2)
    pass_down(chunks - 1)

    bias_kv = [[jnp.zeros((1, HD), F32) for _ in range(HK)] for _ in range(2)]
    for chunk in range(chunks):
        seq, group = chunk // HK, chunk % HK

        @pl.when(core == 0)
        def _():
            exchange(chunk, pair, 0).wait_recv()
            own[chunk] += exch[chunk, pair].astype(F32)

        def incoming(other, _):
            cross(chunk, other, 0).wait_recv()
            own[chunk] += arrive[chunk, other].astype(F32)
            return 0

        lax.fori_loop(pair + 1, pairs, incoming, 0)
        c, s = cos_tab[seq, rows(me), :], sin_tab[seq, rows(me), :]
        key_grad = rope(own[chunk, 0], c, -s).astype(BF16)
        value_grad = own[chunk, 1].astype(BF16)
        gk_ref[seq, :, group * HD:(group + 1) * HD] = key_grad
        gv_ref[seq, :, group * HD:(group + 1) * HD] = value_grad
        bias_kv[0][group] += jnp.sum(key_grad.astype(F32), axis=0, keepdims=True)
        bias_kv[1][group] += jnp.sum(value_grad.astype(F32), axis=0, keepdims=True)
    heads_q = jnp.concatenate([bias_q[group] for group in range(HK)], axis=0)
    for shard in range(fsdps):
        lead = shard * HK // fsdps
        pieces = [heads_q[shard * q_rows:(shard + 1) * q_rows]]
        pieces += bias_kv[0][lead:lead + kv_rows] + bias_kv[1][lead:lead + kv_rows]
        pieces.append(jnp.zeros((bias_rows - q_rows - 2 * kv_rows, HD), F32))
        bias[shard] = jnp.concatenate(pieces, axis=0)

    def over_ctx(step, target):
        return pltpu.make_async_remote_copy(
            bias, bias_in.at[step], b1_send.at[step], b1_recv.at[step],
            device_id=ctx_device(target), device_id_type=MESH)

    for step in range(1, n):
        over_ctx(step, (me + step) % n).start()
    total = bias[...]
    for step in range(1, n):
        over_ctx(step, me).wait_recv()
        total = total + bias_in[step]
    bias_half[...] = total

    def over_rest(step):
        device = far_device(step)
        return pltpu.make_async_remote_copy(
            bias_half.at[device["fsdp"]], bias_half_in.at[step], b2_send.at[step], b2_recv.at[step],
            device_id=device, device_id_type=MESH)

    for step in range(1, others):
        over_rest(step).start()
    final = bias_half[fs]
    for step in range(1, others):
        over_rest(step).wait_recv()
        final = final + bias_half_in[step]
    bq_ref[...] = final[0:q_rows]
    bk_ref[...] = final[q_rows:q_rows + kv_rows]
    bv_ref[...] = final[q_rows + kv_rows:q_rows + 2 * kv_rows]

    def meta_end(target, _):
        for copy in meta_copy(me, target, target):
            copy.wait_send()
        return 0

    lax.fori_loop(me + 1, n, meta_end, 0)

    def end(chunk, _):
        def later(other, _):
            for copy in kv_copy(me, 2 * other + core, other, chunk, kv_send, kv_recv, False):
                copy.wait_send()
            return 0

        lax.fori_loop(pair + 1, pairs, later, 0)

        def earlier(other, _):
            for copy in kv_copy(2 * other + core, buddy, other, chunk, fw_send, fw_recv, True):
                copy.wait_send()
            exchange(chunk, other, 2 * other + 1 - core).wait_send()
            cross(chunk, pair, other).wait_send()
            return 0

        lax.fori_loop(0, pair, earlier, 0)

        @pl.when(core == 0)
        def _():
            for copy in kv_copy(me, buddy, pair, chunk, kv_send, kv_recv, False):
                copy.wait_send()

        @pl.when(core == 1)
        def _():
            exchange(chunk, pair, buddy).wait_send()

        pltpu.make_async_copy(
            gq_out.at[chunk], gq_hbm.at[chunk // HK, :, wide(chunk % HK)], out_sem.at[chunk]).wait()
        return 0

    lax.fori_loop(0, chunks, end, 0)
    for step in range(1, n):
        over_ctx(step, me).wait_send()
    for step in range(1, others):
        over_rest(step).wait_send()


PIECES = 4


def finish(*refs):
    made, wide_hbm = refs[:6], refs[6]
    held, load_sem, store_sem = refs[12:]
    results = refs[6:12]
    seqs = made[0].shape[0]
    span = made[0].shape[2] // PIECES
    loads, stores = [], []
    for piece in range(seqs * PIECES):
        place = (piece // PIECES, slice(None), pl.ds(piece % PIECES * span, span))
        loads.append(pltpu.make_async_copy(made[0].at[place], held.at[piece], load_sem.at[piece]))
        stores.append(pltpu.make_async_copy(held.at[piece], wide_hbm.at[place], store_sem.at[piece]))
    for load in loads:
        load.start()
    for source, result in zip(made[1:], results[1:]):
        result[...] = source[...]
    for load, store in zip(loads, stores):
        load.wait()
        store.start()
    for store in stores:
        store.wait()


def per_device(sizes, *args):
    n, reps, fsdps, seqs, toks = sizes
    length, pairs, chunks = n * toks, n // 2, seqs * HK
    rows, width, others = GROUP * toks, HQ * HD, reps * fsdps
    q_rows, kv_rows, bias_rows = bias_layout(fsdps)
    dma = pltpu.SemaphoreType.DMA
    vmem = pl.BlockSpec(memory_space=pltpu.VMEM)
    anywhere = pl.BlockSpec(memory_space=pl.ANY)
    out = pl.pallas_call(
        functools.partial(kernel, sizes),
        out_shape=(
            jax.ShapeDtypeStruct((seqs, toks, HQ * HD), BF16),
            jax.ShapeDtypeStruct((seqs, toks, HK * HD), BF16),
            jax.ShapeDtypeStruct((seqs, toks, HK * HD), BF16),
            jax.ShapeDtypeStruct((q_rows, HD), F32),
            jax.ShapeDtypeStruct((kv_rows, HD), F32),
            jax.ShapeDtypeStruct((kv_rows, HD), F32),
        ),
        in_specs=[anywhere] * 5 + [vmem] * 4,
        out_specs=(anywhere, vmem, vmem, vmem, vmem, vmem),
        scratch_shapes=[
            pltpu.VMEM((seqs, toks, width), BF16),
            pltpu.VMEM((seqs, toks, width), BF16),
            pltpu.VMEM((seqs, toks, width), BF16),
            pltpu.VMEM((seqs, length, HK * HD), BF16),
            pltpu.VMEM((seqs, length, HK * HD), BF16),
            pltpu.VMEM((n, seqs, toks), jnp.int32),
            pltpu.VMEM((n, seqs, toks), jnp.int32),
            pltpu.VMEM((chunks, rows, HD), BF16),
            pltpu.VMEM((chunks, rows, HD), BF16),
            pltpu.VMEM((chunks, 8, rows), F32),
            pltpu.VMEM((seqs, length, HD), F32),
            pltpu.VMEM((seqs, length, HD), F32),
            pltpu.VMEM((seqs, length, rows), F32),
            pltpu.VMEM((chunks, toks, GROUP * HD), BF16),
            pltpu.VMEM((chunks, n, 2, toks, HD), BF16),
            pltpu.VMEM((chunks, 2, toks, HD), F32),
            pltpu.VMEM((chunks, pairs, 2, toks, HD), BF16),
            pltpu.VMEM((chunks, pairs, 2, toks, HD), BF16),
            pltpu.VMEM((chunks, pairs, 2, toks, HD), BF16),
            pltpu.VMEM((HK, GROUP, HD), F32),
            pltpu.VMEM((fsdps, bias_rows, HD), F32),
            pltpu.VMEM((n, fsdps, bias_rows, HD), F32),
            pltpu.VMEM((fsdps, bias_rows, HD), F32),
            pltpu.VMEM((others, bias_rows, HD), F32),
            dma((5, seqs)),
            dma((chunks,)),
            dma((2, n)),
            dma((2, n)),
            dma((2, pairs, chunks)),
            dma((2, n, chunks)),
            dma((2, pairs, chunks)),
            dma((2, n, chunks)),
            dma((chunks, pairs)),
            dma((chunks, pairs)),
            dma((chunks, pairs)),
            dma((chunks, pairs)),
            dma((n,)),
            dma((n,)),
            dma((others,)),
            dma((others,)),
        ],
        compiler_params=pltpu.CompilerParams(
            collective_id=0, has_side_effects=True, vmem_limit_bytes=60 * 1024 * 1024
        ),
        name="attention_backward",
    )(*args)
    out = pl.pallas_call(
        finish,
        out_shape=tuple(jax.ShapeDtypeStruct(part.shape, part.dtype) for part in out),
        in_specs=[anywhere] + [vmem] * 5,
        out_specs=(anywhere,) + (vmem,) * 5,
        scratch_shapes=[
            pltpu.VMEM((seqs * PIECES, toks, width // PIECES), BF16),
            dma((seqs * PIECES,)),
            dma((seqs * PIECES,)),
        ],
        name="finish",
    )(*out)
    flat = [part.reshape(-1) for part in out[3:]]
    share = HK * HD // fsdps
    if share < HD:
        begin = (lax.axis_index("fsdp") * share) % HD
        flat[1:] = [lax.dynamic_slice(part, (begin,), (share,)) for part in flat[1:]]
    return out[:3] + tuple(flat)


def solution(mesh):
    tokens = P(("rep", "fsdp"), "ctx", None)
    flat = P(("rep", "fsdp"), "ctx")
    shape = dict(mesh.shape)

    def run(*args):
        n, reps, fsdps = shape["ctx"], shape["rep"], shape["fsdp"]
        sizes = (n, reps, fsdps, args[0].shape[0] // (reps * fsdps), args[0].shape[1] // n)
        return jax.shard_map(
            functools.partial(per_device, sizes),
            mesh=mesh,
            in_specs=(tokens,) * 5 + (flat,) * 4,
            out_specs=(tokens, tokens, tokens, P("fsdp"), P("fsdp"), P("fsdp")),
            check_vma=False,
        )(*args)

    return run
```
